32 devices in a mesh: dp: 4 (over y, core), slab: 8 (over z, x).
Axes of the slice: x: 2, y: 2, z: 4, core: 2. Of those that a mesh axis runs over, the one named last changes fastest.
Arguments:
- features: bfloat16 [4, 64, 256, 8, 256], P('dp', None, 'slab'), may hold values from -6 to 6
- target: bfloat16 [4, 256, 8, 256], P('dp', 'slab'), may hold values from -6 to 6
- out_weight: float32 [64], replicated, may hold values from -1.5 to 1.5
- rotation: int32 [4], P('dp'), may hold values from 0 to 3
- blocks: int32 [8, 2], replicated, may hold values from 0 to 3, as said below
- wedge: int32 [256, 256], replicated, may hold values 0 or 1
Outputs:
- vol_grad: float32 [4, 256, 8, 256], P('dp', 'slab')
- w_grad: float32 [64], replicated
The draws below stay inside these ranges and needn't reach their ends.
Inputs may be any that keep to these rules, and one draw needn't show every extreme that they name: `blocks`: the 8 rows are distinct pairs of block indices of the frequency plane, each from 0 to 3.
All inputs are finite; a program needn't handle non-finite values.
Results may differ from the reference program's by a relative error of at most 0.0003.
Values sent between devices are 32-bit elements; how exact they have to be, the bound alone decides.
A program may use at most 64 MiB of HBM per device.

```python
import jax
import jax.numpy as jnp
from jax import lax

C = 64
N = 256
BLK = 64
NB = 8
YP = 8
SAMPLES = 4


def draw_blocks(key, part):
    per_side = N // BLK
    picked = jax.random.permutation(key, per_side * per_side)[:NB]
    return jnp.stack([picked // per_side, picked % per_side], axis=1).astype(jnp.int32)


def place_ends(drawn, stream_key, smallest, top_value):
    longest = drawn.shape.index(max(drawn.shape))
    spots = []
    for shift in (0, 1):
        where = [jax.random.randint(jax.random.fold_in(stream_key, axis), (), 0, length) for axis, length in enumerate(drawn.shape)]
        where[longest] = (where[longest] + shift) % drawn.shape[longest]
        spots.append(tuple(where))
    return drawn.at[spots[0]].set(smallest).at[spots[1]].set(top_value)


def steps_of(own_key, extent, split, low, largest):
    factor_of = 1.0
    for dim, shards_of in split:
        heights = jax.random.uniform(jax.random.fold_in(jax.random.fold_in(own_key, 6), dim), (shards_of,), jnp.float32, low / len(split), largest / len(split))
        factor_of = factor_of * jnp.repeat(jnp.exp(heights), extent[dim] // shards_of).reshape((-1,) + (1,) * (len(extent) - 1 - dim))
    return factor_of


def centred(own_key, dims, deviation, most, cuts=(), kind=jnp.bfloat16):
    values = deviation * jax.random.normal(own_key, dims, jnp.float32)
    if cuts:
        values = values * steps_of(own_key, dims, cuts, -0.22, 0.18)
    return jnp.clip(values, -most, most).astype(kind)


def setup_inputs(seed: int = 0) -> dict:
    streams_of = jax.random.split(jax.random.key(seed), 7)
    return {
        "features": centred(streams_of[0], (SAMPLES, C, N, YP, N), 1.0, 6.0, ((0, 4), (2, 8))),
        "target": centred(streams_of[1], (SAMPLES, N, YP, N), 1.0, 6.0, ((0, 4), (1, 8))),
        "out_weight": centred(streams_of[2], (C,), 0.25, 1.5, (), jnp.float32),
        "rotation": place_ends(jax.random.randint(streams_of[3], (SAMPLES,), 0, 4), jax.random.fold_in(streams_of[3], 1), 0, 3).astype(jnp.int32),
        "blocks": draw_blocks(jax.random.fold_in(streams_of[6], 71), 0),
        "wedge": place_ends((jax.random.randint(streams_of[5], (N, N), 0, 5) < 3).astype(jnp.int32), jax.random.fold_in(streams_of[5], 1), 0, 1),
    }


def turned(volume, turns):
    result = volume
    for count in range(1, 4):
        result = jnp.where(turns == count, jnp.rot90(volume, count, axes=(0, 2)), result)
    return result


def wedge_weights(blocks, wedge):
    per_side = N // BLK
    labels = jnp.arange(per_side, dtype=jnp.int32)
    match = (blocks[:, 0][:, None, None] == labels[None, :, None]) & (blocks[:, 1][:, None, None] == labels[None, None, :])
    listed = jnp.any(match, axis=0)
    spread = jnp.repeat(jnp.repeat(listed, BLK, axis=0), BLK, axis=1)
    return jnp.where(spread, wedge, 0).astype(jnp.float32)


def reference(features, target, out_weight, rotation, blocks, wedge):
    mask = wedge_weights(blocks, wedge)

    def single(items):
        sample, other, turns = items
        wide = sample.astype(jnp.float32)
        volume = jnp.einsum("c,czyx->zyx", out_weight, wide, precision=lax.Precision.HIGHEST)
        difference = volume - other.astype(jnp.float32)
        rotated = turned(difference, turns)
        spectrum = jnp.fft.fft2(rotated, axes=(0, 2)) / N
        grad_spectrum = 2.0 * mask[:, None, :] * spectrum
        rot_grad = N * jnp.real(jnp.fft.ifft2(grad_spectrum, axes=(0, 2)))
        back = turned(rot_grad, (4 - turns) % 4).astype(jnp.float32)
        piece = jnp.einsum("czyx,zyx->c", wide, back, precision=lax.Precision.HIGHEST)
        return back, piece.astype(jnp.float32)

    vol_grad, pieces = lax.map(single, (features, target, rotation))
    w_grad = jnp.sum(pieces, axis=0) / (SAMPLES * N * YP * N)
    return vol_grad, w_grad
```

```python
import functools
import math

import numpy as np

import jax
import jax.numpy as jnp
from jax import lax
from jax.experimental import pallas as pl
from jax.experimental.pallas import tpu as pltpu
from jax.sharding import PartitionSpec as P

BLK = 64
ROWS = 8
MESH = pl.DeviceIdType.MESH


def product(form, left, right):
    return jnp.einsum(form, left, right, precision=lax.Precision.HIGHEST)


def wedge_weights(blocks, wedge, length):
    per_side = length // BLK
    labels = jnp.arange(per_side, dtype=jnp.int32)
    match = (blocks[:, 0][:, None, None] == labels[None, :, None]) & (
        blocks[:, 1][:, None, None] == labels[None, None, :]
    )
    listed = jnp.any(match, axis=0)
    spread = jnp.repeat(jnp.repeat(listed, BLK, axis=0), BLK, axis=1)
    return jnp.where(spread, wedge, 0).astype(jnp.float32)


def phase_tables(turns, length):
    positions = jnp.arange(length, dtype=jnp.int32)
    flip_depth = turns >= 2
    flip_width = (turns == 1) | (turns == 2)
    depth_index = jnp.where(
        flip_depth[:, None], length - 1 - positions[None, :], positions[None, :]
    )
    width_index = jnp.where(
        flip_width[:, None], length - 1 - positions[None, :], positions[None, :]
    )
    depth_phase = positions[None, :, None] * depth_index[:, None, :] % length
    width_phase = width_index[:, :, None] * positions[None, None, :] % length
    depth_angle = depth_phase.astype(jnp.float32) * (2.0 * math.pi / length)
    width_angle = width_phase.astype(jnp.float32) * (2.0 * math.pi / length)
    return (jnp.cos(depth_angle), jnp.sin(depth_angle), jnp.cos(width_angle), jnp.sin(width_angle))


def split_lines(features, target, out_weight, rotation, blocks, wedge):
    length = features.shape[-1]
    plane_count = features.shape[3]
    slab_count = lax.axis_size("slab")
    columns = length // slab_count
    col_start = lax.axis_index("slab") * columns
    features_wide = features.astype(jnp.float32)
    volume = product("c,sczyx->szyx", out_weight, features_wide)
    difference = volume - target.astype(jnp.float32)
    depth_cos, depth_sin, width_cos, width_sin = phase_tables(rotation, length)
    line_real = product("szyb,sbp->szyp", difference, width_cos)
    line_imag = -product("szyb,sbp->szyp", difference, width_sin)
    line_real, line_imag = (
        lax.all_to_all(line_real, "slab", split_axis=3, concat_axis=1, tiled=True),
        lax.all_to_all(line_imag, "slab", split_axis=3, concat_axis=1, tiled=True),
    )
    spec_real = (
        product("spa,sayq->spyq", depth_cos, line_real)
        + product("spa,sayq->spyq", depth_sin, line_imag)
    ) / length
    spec_imag = (
        product("spa,sayq->spyq", depth_cos, line_imag)
        - product("spa,sayq->spyq", depth_sin, line_real)
    ) / length
    mask = wedge_weights(blocks, wedge, length)
    odd_turn = rotation % 2 == 1
    mask_turned = jnp.where(odd_turn[:, None, None], mask.T[None], mask[None])
    mask_columns = lax.dynamic_slice_in_dim(mask_turned, col_start, columns, 2)
    grad_real = 2.0 * mask_columns[:, :, None, :] * spec_real
    grad_imag = 2.0 * mask_columns[:, :, None, :] * spec_imag
    back_real = product("spa,spyq->sayq", depth_cos, grad_real) - product(
        "spa,spyq->sayq", depth_sin, grad_imag
    )
    back_imag = product("spa,spyq->sayq", depth_cos, grad_imag) + product(
        "spa,spyq->sayq", depth_sin, grad_real
    )
    back_real, back_imag = (
        lax.all_to_all(back_real, "slab", split_axis=1, concat_axis=3, tiled=True),
        lax.all_to_all(back_imag, "slab", split_axis=1, concat_axis=3, tiled=True),
    )
    vol_grad = (
        product("sayp,sbp->sayb", back_real, width_cos)
        - product("sayp,sbp->sayb", back_imag, width_sin)
    ) / length
    voxel_count = lax.axis_size("dp") * features.shape[0] * length * plane_count * length
    local_sum = product("sczyx,szyx->c", features_wide, vol_grad) / voxel_count
    w_grad = lax.psum(local_sum, ("dp", "slab"))
    return (vol_grad, w_grad)


def hartley_tables(length):
    index = np.arange(length)
    angle = (index[:, None] * index[None, :] % length) * (2.0 * np.pi / length)
    cos, sin = np.cos(angle), np.sin(angle)
    parts = []
    for table in (cos, sin, cos + sin, cos - sin):
        high = table.astype(jnp.bfloat16)
        parts += [high, (table - high.astype(np.float64)).astype(jnp.bfloat16)]
    return np.stack(parts)


def halves(value):
    high = value.astype(jnp.bfloat16)
    return high, (value - high.astype(jnp.float32)).astype(jnp.bfloat16)


def dot(left, right):
    return jnp.dot(left, right, preferred_element_type=jnp.float32)


def dot3(left, right):
    return dot(left[0], right[0]) + (dot(left[0], right[1]) + dot(left[1], right[0]))


def kernel(
    dp_count, slab_count, voxel_count,
    weight, rotation, blocks, features_hbm, target_hbm, wedge_hbm, tables_hbm,
    out, out_weight_grad,
    features, target, wedge, tables, outgoing, plane, filt, back, returned, sums, own_sum, all_sums,
    load_sem, side_sem, send_sem, recv_sem, send2_sem, recv2_sem, sum_send_sem, sum_recv_sem,
):
    channels, depth, planes, length = features.shape
    pieces = depth // ROWS
    my_dp, me = lax.axis_index("dp"), lax.axis_index("slab")
    total = dp_count * slab_count

    def other(offset):
        place = lax.rem(my_dp * slab_count + me + offset, total)
        return (lax.div(place, slab_count), lax.rem(place, slab_count))

    loads = []
    for j in range(pieces):
        rows = pl.ds(j * ROWS, ROWS)
        loads.append(pltpu.make_async_copy(features_hbm.at[:, rows], features.at[:, rows], load_sem.at[j]))
    sides = [
        pltpu.make_async_copy(target_hbm, target, side_sem.at[0]),
        pltpu.make_async_copy(wedge_hbm, wedge, side_sem.at[1]),
        pltpu.make_async_copy(tables_hbm, tables, side_sem.at[2]),
    ]
    sides[0].start()
    for copy in loads:
        copy.start()
    for copy in sides[1:]:
        copy.start()

    barrier = pltpu.get_barrier_semaphore()
    for offset in range(1, total):
        pl.semaphore_signal(barrier, inc=1, device_id=other(offset), device_id_type=MESH)

    sends = []
    for j in range(pieces):
        loads[j].wait()
        if j == 0:
            sides[0].wait()
        base = j * ROWS

        def add_channel(c, accs):
            scale = weight[c]
            return tuple(
                accs[z] + scale * features[c, base + z].astype(jnp.float32) for z in range(ROWS)
            )

        start = tuple(-target[base + z].astype(jnp.float32) for z in range(ROWS))
        accs = lax.fori_loop(0, channels, add_channel, start, unroll=4)
        piece = jnp.swapaxes(jnp.stack(accs, axis=0), 0, 1)
        outgoing[:, pl.ds(base, ROWS), :] = piece
        if j == 0:
            pl.semaphore_wait(barrier, total - 1)
        for r in range(1, slab_count):
            peer = lax.rem(me + r, slab_count)
            copy = pltpu.make_async_remote_copy(
                src_ref=outgoing.at[peer, pl.ds(base, ROWS)],
                dst_ref=plane.at[pl.ds(pl.multiple_of(me * depth + base, ROWS), ROWS)],
                send_sem=send_sem.at[r - 1, j],
                recv_sem=recv_sem.at[r - 1, j],
                device_id=(my_dp, peer),
                device_id_type=MESH,
            )
            copy.start()
            sends.append(copy)
        plane[pl.ds(pl.multiple_of(me * depth + base, ROWS), ROWS), :] = outgoing[me, pl.ds(base, ROWS), :]

    sides[1].wait()
    row = lax.broadcasted_iota(jnp.int32, (length, length), 0)
    column = lax.broadcasted_iota(jnp.int32, (length, length), 1)
    row_block, column_block = row // BLK, column // BLK
    listed = jnp.zeros((length, length), jnp.bool_)
    for n in range(blocks.shape[1]):
        listed = listed | ((row_block == blocks[0, n]) & (column_block == blocks[1, n]))
    mask = jnp.where(listed, wedge[...], 0).astype(jnp.float32)
    mirror = jnp.where(lax.rem(row + column, length) == 0, 1.0, 0.0).astype(jnp.bfloat16)
    flipped = dot(dot(mirror, mask.astype(jnp.bfloat16)).astype(jnp.bfloat16), mirror)
    even = mask + flipped
    odd = lax.dot_general(
        even.astype(jnp.bfloat16), mirror, (((0,), (0,)), ((), ())), preferred_element_type=jnp.float32
    )
    is_odd = lax.rem(rotation[0], 2) == 1
    filt[...] = jnp.where(is_odd, odd, even) * (1.0 / (length * length))
    sides[2].wait()

    for copy in sends:
        copy.wait()

    def table(k):
        return tables[2 * k], tables[2 * k + 1]

    values = halves(plane[...])
    first, second = halves(dot3(values, table(2))), halves(dot3(values, table(3)))
    spectrum = dot3(table(0), first) + dot3(table(1), second)
    kept = halves(spectrum * filt[...])
    first, second = halves(dot3(table(0), kept)), halves(dot3(table(1), kept))
    back[...] = dot3(first, table(2)) + dot3(second, table(3))

    sends = []
    for r in range(1, slab_count):
        peer = lax.rem(me + r, slab_count)
        copy = pltpu.make_async_remote_copy(
            src_ref=back.at[pl.ds(pl.multiple_of(peer * depth, ROWS), depth)],
            dst_ref=returned.at[me],
            send_sem=send2_sem.at[r - 1],
            recv_sem=recv2_sem.at[r - 1],
            device_id=(my_dp, peer),
            device_id_type=MESH,
        )
        copy.start()
        sends.append(copy)
    returned[me] = back[pl.ds(pl.multiple_of(me * depth, ROWS), depth), :]
    for copy in sends:
        copy.wait()

    for j in range(pieces):
        base = j * ROWS
        piece = jnp.swapaxes(returned[:, pl.ds(base, ROWS), :], 0, 1)
        out[pl.ds(base, ROWS)] = piece
        grads = [piece[z] for z in range(ROWS)]

        def channel_sum(c, carry):
            acc = grads[0] * features[c, base].astype(jnp.float32)
            for z in range(1, ROWS):
                acc = acc + grads[z] * features[c, base + z].astype(jnp.float32)
            folded = acc[:, :128]
            for lane in range(128, length, 128):
                folded = folded + acc[:, lane:lane + 128]
            sums[c] = folded if j == 0 else sums[c] + folded
            return carry

        lax.fori_loop(0, channels, channel_sum, 0, unroll=4)

    rest = jnp.sum(sums[...], axis=1)
    ones = jnp.ones((8, 128), jnp.bfloat16)
    row_sum = jnp.zeros((8, channels), jnp.float32)
    for _ in range(3):
        part = rest.astype(jnp.bfloat16)
        rest = rest - part.astype(jnp.float32)
        row_sum = row_sum + lax.dot_general(
            ones, part, (((1,), (1,)), ((), ())), preferred_element_type=jnp.float32
        )
    row_sum = row_sum[0:1]
    own_sum[0] = row_sum
    place = my_dp * slab_count + me
    sends = []
    for offset in range(1, total):
        copy = pltpu.make_async_remote_copy(
            src_ref=own_sum.at[0],
            dst_ref=all_sums.at[place],
            send_sem=sum_send_sem.at[offset - 1],
            recv_sem=sum_recv_sem.at[offset - 1],
            device_id=other(offset),
            device_id_type=MESH,
        )
        copy.start()
        sends.append(copy)
    all_sums[place] = row_sum
    for copy in sends:
        copy.wait()
    out_weight_grad[...] = jnp.sum(all_sums[...], axis=0) / voxel_count


def split_planes(features, target, out_weight, rotation, blocks, wedge):
    _, channels, depth, planes, length = features.shape
    dp_count, slab_count = lax.axis_size("dp"), lax.axis_size("slab")
    total = dp_count * slab_count
    pieces = depth // ROWS
    voxel_count = dp_count * length * planes * length
    smem = pl.BlockSpec(memory_space=pltpu.SMEM)
    hbm = pl.BlockSpec(memory_space=pltpu.HBM)
    vmem = pl.BlockSpec(memory_space=pltpu.VMEM)
    dma = pltpu.SemaphoreType.DMA
    vol_grad, w_grad = pl.pallas_call(
        functools.partial(kernel, dp_count, slab_count, float(voxel_count)),
        out_shape=(
            jax.ShapeDtypeStruct((depth, planes, length), jnp.float32),
            jax.ShapeDtypeStruct((1, channels), jnp.float32),
        ),
        in_specs=[smem, smem, smem, hbm, hbm, hbm, hbm],
        out_specs=(vmem, vmem),
        scratch_shapes=[
            pltpu.VMEM((channels, depth, planes, length), jnp.bfloat16),
            pltpu.VMEM((depth, planes, length), jnp.bfloat16),
            pltpu.VMEM((length, length), jnp.int32),
            pltpu.VMEM((8, length, length), jnp.bfloat16),
            pltpu.VMEM((planes, depth, length), jnp.float32),
            pltpu.VMEM((length, length), jnp.float32),
            pltpu.VMEM((length, length), jnp.float32),
            pltpu.VMEM((length, length), jnp.float32),
            pltpu.VMEM((planes, depth, length), jnp.float32),
            pltpu.VMEM((channels, 8, 128), jnp.float32),
            pltpu.VMEM((1, 1, channels), jnp.float32),
            pltpu.VMEM((total, 1, channels), jnp.float32),
            dma((pieces,)),
            dma((3,)),
            dma((slab_count - 1, pieces)),
            dma((slab_count - 1, pieces)),
            dma((slab_count - 1,)),
            dma((slab_count - 1,)),
            dma((total - 1,)),
            dma((total - 1,)),
        ],
        compiler_params=pltpu.CompilerParams(
            collective_id=0, has_side_effects=True, vmem_limit_bytes=56 * 1024 * 1024
        ),
    )(
        out_weight, rotation, blocks.T, features[0], target[0], wedge, jnp.asarray(hartley_tables(length)),
    )
    return vol_grad[None], w_grad[0]


def solution(mesh):
    def on_device(features, *rest):
        samples, _, depth, planes, length = features.shape
        whole_planes = (
            samples == 1
            and planes == 8
            and planes == mesh.shape["slab"]
            and depth % ROWS == 0
            and length % 128 == 0
        )
        return (split_planes if whole_planes else split_lines)(features, *rest)

    in_specs = (
        P("dp", None, "slab", None, None),
        P("dp", "slab", None, None),
        P(),
        P("dp"),
        P(),
        P(),
    )
    out_specs = (P("dp", "slab", None, None), P())
    return jax.shard_map(
        on_device, mesh=mesh, in_specs=in_specs, out_specs=out_specs, check_vma=False
    )
```

```python
import functools
import math

import numpy as np

import jax
import jax.numpy as jnp
from jax import lax
from jax.experimental import pallas as pl
from jax.experimental.pallas import tpu as pltpu
from jax.sharding import PartitionSpec as P

BLK = 64
ROWS = 8
HELD = 2
MESH = pl.DeviceIdType.MESH


def product(form, left, right):
    return jnp.einsum(form, left, right, precision=lax.Precision.HIGHEST)


def wedge_weights(blocks, wedge, length):
    per_side = length // BLK
    labels = jnp.arange(per_side, dtype=jnp.int32)
    match = (blocks[:, 0][:, None, None] == labels[None, :, None]) & (
        blocks[:, 1][:, None, None] == labels[None, None, :]
    )
    listed = jnp.any(match, axis=0)
    spread = jnp.repeat(jnp.repeat(listed, BLK, axis=0), BLK, axis=1)
    return jnp.where(spread, wedge, 0).astype(jnp.float32)


def phase_tables(turns, length):
    positions = jnp.arange(length, dtype=jnp.int32)
    flip_depth = turns >= 2
    flip_width = (turns == 1) | (turns == 2)
    depth_index = jnp.where(
        flip_depth[:, None], length - 1 - positions[None, :], positions[None, :]
    )
    width_index = jnp.where(
        flip_width[:, None], length - 1 - positions[None, :], positions[None, :]
    )
    depth_phase = positions[None, :, None] * depth_index[:, None, :] % length
    width_phase = width_index[:, :, None] * positions[None, None, :] % length
    depth_angle = depth_phase.astype(jnp.float32) * (2.0 * math.pi / length)
    width_angle = width_phase.astype(jnp.float32) * (2.0 * math.pi / length)
    return (jnp.cos(depth_angle), jnp.sin(depth_angle), jnp.cos(width_angle), jnp.sin(width_angle))


def split_lines(features, target, out_weight, rotation, blocks, wedge):
    length = features.shape[-1]
    plane_count = features.shape[3]
    slab_count = lax.axis_size("slab")
    columns = length // slab_count
    col_start = lax.axis_index("slab") * columns
    features_wide = features.astype(jnp.float32)
    volume = product("c,sczyx->szyx", out_weight, features_wide)
    difference = volume - target.astype(jnp.float32)
    depth_cos, depth_sin, width_cos, width_sin = phase_tables(rotation, length)
    line_real = product("szyb,sbp->szyp", difference, width_cos)
    line_imag = -product("szyb,sbp->szyp", difference, width_sin)
    line_real, line_imag = (
        lax.all_to_all(line_real, "slab", split_axis=3, concat_axis=1, tiled=True),
        lax.all_to_all(line_imag, "slab", split_axis=3, concat_axis=1, tiled=True),
    )
    spec_real = (
        product("spa,sayq->spyq", depth_cos, line_real)
        + product("spa,sayq->spyq", depth_sin, line_imag)
    ) / length
    spec_imag = (
        product("spa,sayq->spyq", depth_cos, line_imag)
        - product("spa,sayq->spyq", depth_sin, line_real)
    ) / length
    mask = wedge_weights(blocks, wedge, length)
    odd_turn = rotation % 2 == 1
    mask_turned = jnp.where(odd_turn[:, None, None], mask.T[None], mask[None])
    mask_columns = lax.dynamic_slice_in_dim(mask_turned, col_start, columns, 2)
    grad_real = 2.0 * mask_columns[:, :, None, :] * spec_real
    grad_imag = 2.0 * mask_columns[:, :, None, :] * spec_imag
    back_real = product("spa,spyq->sayq", depth_cos, grad_real) - product(
        "spa,spyq->sayq", depth_sin, grad_imag
    )
    back_imag = product("spa,spyq->sayq", depth_cos, grad_imag) + product(
        "spa,spyq->sayq", depth_sin, grad_real
    )
    back_real, back_imag = (
        lax.all_to_all(back_real, "slab", split_axis=1, concat_axis=3, tiled=True),
        lax.all_to_all(back_imag, "slab", split_axis=1, concat_axis=3, tiled=True),
    )
    vol_grad = (
        product("sayp,sbp->sayb", back_real, width_cos)
        - product("sayp,sbp->sayb", back_imag, width_sin)
    ) / length
    voxel_count = lax.axis_size("dp") * features.shape[0] * length * plane_count * length
    local_sum = product("sczyx,szyx->c", features_wide, vol_grad) / voxel_count
    w_grad = lax.psum(local_sum, ("dp", "slab"))
    return (vol_grad, w_grad)


def hartley_tables(length):
    index = np.arange(length)
    angle = (index[:, None] * index[None, :] % length) * (2.0 * np.pi / length)
    cos, sin = np.cos(angle), np.sin(angle)
    parts = []
    for table in (cos, sin, cos + sin, cos - sin):
        high = table.astype(jnp.bfloat16)
        parts += [high, (table - high.astype(np.float64)).astype(jnp.bfloat16)]
    return np.stack(parts)


def halves(value):
    high = value.astype(jnp.bfloat16)
    return high, (value - high.astype(jnp.float32)).astype(jnp.bfloat16)


def dot(left, right):
    return jnp.dot(left, right, preferred_element_type=jnp.float32)


def dot3(left, right):
    return dot(left[0], right[0]) + (dot(left[0], right[1]) + dot(left[1], right[0]))


def kernel(
    dp_count, slab_count, voxel_count,
    weight, rotation, blocks, features_hbm, target_hbm, wedge_hbm, tables_hbm,
    out_hbm, out_sums,
    features, target, wedge, tables, out, outgoing, plane, filt, back, returned, sums, own_sum, slab_sums, dp_sums,
    load_sem, side_sem, send_sem, recv_sem, send2_sem, recv2_sem, sum_send_sem, sum_recv_sem, dp_send_sem, dp_recv_sem,
):
    channels, depth, planes, length = features.shape
    pieces = depth // ROWS
    my_dp, me = lax.axis_index("dp"), lax.axis_index("slab")
    slab_steps = range(slab_count - 1, 0, -1)

    def slab_peer(step):
        return lax.bitwise_xor(me, jnp.int32(step))

    def dp_peer(step):
        return lax.rem(my_dp + step, dp_count)

    loads = []
    for j in range(pieces):
        rows = pl.ds(j * ROWS, ROWS)
        loads.append(pltpu.make_async_copy(features_hbm.at[:, rows], features.at[:, rows], load_sem.at[j]))
    sides = [
        pltpu.make_async_copy(target_hbm, target, side_sem.at[0]),
        pltpu.make_async_copy(wedge_hbm, wedge, side_sem.at[1]),
        pltpu.make_async_copy(tables_hbm, tables, side_sem.at[2]),
    ]
    sides[0].start()
    for copy in loads:
        copy.start()
    for copy in sides[1:]:
        copy.start()

    barrier = pltpu.get_barrier_semaphore()
    for r in slab_steps:
        pl.semaphore_signal(barrier, inc=1, device_id=(my_dp, slab_peer(r)), device_id_type=MESH)
    for r in range(1, dp_count):
        pl.semaphore_signal(barrier, inc=1, device_id=(dp_peer(r), me), device_id_type=MESH)

    sends = []
    for j in range(pieces):
        loads[j].wait()
        if j == 0:
            sides[0].wait()
        base = j * ROWS

        def add_channel(c, accs):
            scale = weight[c]
            return tuple(
                accs[z] + scale * features[c, base + z].astype(jnp.float32) for z in range(ROWS)
            )

        start = tuple(-target[base + z].astype(jnp.float32) for z in range(ROWS))
        accs = lax.fori_loop(0, channels, add_channel, start, unroll=4)
        piece = jnp.swapaxes(jnp.stack(accs, axis=0), 0, 1)
        outgoing[:, pl.ds(base, ROWS), :] = piece
        plane[pl.ds(pl.multiple_of(me * depth + base, ROWS), ROWS), :] = outgoing[me, pl.ds(base, ROWS), :]
        if j < min(HELD, pieces) - 1:
            continue
        first = j
        if j == min(HELD, pieces) - 1:
            pl.semaphore_wait(barrier, slab_count + dp_count - 2)
            first = 0
        rows = pl.ds(first * ROWS, (j + 1 - first) * ROWS)
        for r in slab_steps:
            peer = slab_peer(r)
            copy = pltpu.make_async_remote_copy(
                src_ref=outgoing.at[peer, rows],
                dst_ref=plane.at[pl.ds(pl.multiple_of(me * depth + first * ROWS, ROWS), (j + 1 - first) * ROWS)],
                send_sem=send_sem.at[r - 1, j],
                recv_sem=recv_sem.at[r - 1, j],
                device_id=(my_dp, peer),
                device_id_type=MESH,
            )
            copy.start()
            sends.append(copy)

    sides[1].wait()
    row = lax.broadcasted_iota(jnp.int32, (length, length), 0)
    column = lax.broadcasted_iota(jnp.int32, (length, length), 1)
    row_block, column_block = row // BLK, column // BLK
    listed = jnp.zeros((length, length), jnp.bool_)
    for n in range(blocks.shape[1]):
        listed = listed | ((row_block == blocks[0, n]) & (column_block == blocks[1, n]))
    mask = jnp.where(listed, wedge[...], 0).astype(jnp.float32)
    mirror = jnp.where(lax.rem(row + column, length) == 0, 1.0, 0.0).astype(jnp.bfloat16)
    flipped = dot(dot(mirror, mask.astype(jnp.bfloat16)).astype(jnp.bfloat16), mirror)
    even = mask + flipped
    odd = lax.dot_general(
        even.astype(jnp.bfloat16), mirror, (((0,), (0,)), ((), ())), preferred_element_type=jnp.float32
    )
    is_odd = lax.rem(rotation[0], 2) == 1
    filt[...] = jnp.where(is_odd, odd, even) * (1.0 / (length * length))
    sides[2].wait()

    for copy in sends:
        copy.wait()

    def table(k):
        return tables[2 * k], tables[2 * k + 1]

    values = halves(plane[...])
    first, second = halves(dot3(values, table(2))), halves(dot3(values, table(3)))
    spectrum = dot3(table(0), first) + dot3(table(1), second)
    kept = halves(spectrum * filt[...])
    first, second = halves(dot3(table(0), kept)), halves(dot3(table(1), kept))
    back[...] = dot3(first, table(2)) + dot3(second, table(3))

    sends = []
    for j in range(pieces):
        sends.append([])
        for r in slab_steps:
            peer = slab_peer(r)
            copy = pltpu.make_async_remote_copy(
                src_ref=back.at[pl.ds(pl.multiple_of(peer * depth + j * ROWS, ROWS), ROWS)],
                dst_ref=returned.at[me, pl.ds(j * ROWS, ROWS)],
                send_sem=send2_sem.at[r - 1, j],
                recv_sem=recv2_sem.at[r - 1, j],
                device_id=(my_dp, peer),
                device_id_type=MESH,
            )
            copy.start()
            sends[j].append(copy)
    returned[me] = back[pl.ds(pl.multiple_of(me * depth, ROWS), depth), :]

    for j in range(pieces):
        base = j * ROWS
        for copy in sends[j]:
            copy.wait()
        piece = jnp.swapaxes(returned[:, pl.ds(base, ROWS), :], 0, 1)
        out[pl.ds(base, ROWS)] = piece
        grads = [piece[z] for z in range(ROWS)]

        def channel_sum(c, carry):
            acc = grads[0] * features[c, base].astype(jnp.float32)
            for z in range(1, ROWS):
                acc = acc + grads[z] * features[c, base + z].astype(jnp.float32)
            folded = acc[:, :128]
            for lane in range(128, length, 128):
                folded = folded + acc[:, lane:lane + 128]
            sums[c] = folded if j == 0 else sums[c] + folded
            return carry

        lax.fori_loop(0, channels, channel_sum, 0, unroll=4)
    stored = pltpu.make_async_copy(out, out_hbm, side_sem.at[3])
    stored.start()

    rest = jnp.sum(sums[...], axis=1)
    ones = jnp.ones((8, 128), jnp.bfloat16)
    row_sum = jnp.zeros((8, channels), jnp.float32)
    for _ in range(3):
        part = rest.astype(jnp.bfloat16)
        rest = rest - part.astype(jnp.float32)
        row_sum = row_sum + lax.dot_general(
            ones, part, (((1,), (1,)), ((), ())), preferred_element_type=jnp.float32
        )
    row_sum = row_sum[0:1]
    own_sum[0] = row_sum
    sends = []
    for r in slab_steps:
        copy = pltpu.make_async_remote_copy(
            src_ref=own_sum.at[0],
            dst_ref=slab_sums.at[me],
            send_sem=sum_send_sem.at[r - 1],
            recv_sem=sum_recv_sem.at[r - 1],
            device_id=(my_dp, slab_peer(r)),
            device_id_type=MESH,
        )
        copy.start()
        sends.append(copy)
    slab_sums[me] = row_sum
    for copy in sends:
        copy.wait()
    row_sum = jnp.sum(slab_sums[...], axis=0)
    own_sum[1] = row_sum
    sends = []
    for r in range(1, dp_count):
        copy = pltpu.make_async_remote_copy(
            src_ref=own_sum.at[1],
            dst_ref=dp_sums.at[my_dp],
            send_sem=dp_send_sem.at[r - 1],
            recv_sem=dp_recv_sem.at[r - 1],
            device_id=(dp_peer(r), me),
            device_id_type=MESH,
        )
        copy.start()
        sends.append(copy)
    dp_sums[my_dp] = row_sum
    for copy in sends:
        copy.wait()
    out_sums[...] = jnp.sum(dp_sums[...], axis=0) / voxel_count
    stored.wait()


def hand_over(vol_grad, w_grad, out, out_weight_grad):
    out[...] = vol_grad[...]
    out_weight_grad[...] = w_grad[...]


def split_planes(features, target, out_weight, rotation, blocks, wedge):
    _, channels, depth, planes, length = features.shape
    dp_count, slab_count = lax.axis_size("dp"), lax.axis_size("slab")
    pieces = depth // ROWS
    voxel_count = dp_count * length * planes * length
    smem = pl.BlockSpec(memory_space=pltpu.SMEM)
    hbm = pl.BlockSpec(memory_space=pltpu.HBM)
    vmem = pl.BlockSpec(memory_space=pltpu.VMEM)
    dma = pltpu.SemaphoreType.DMA
    vol_grad, w_grad = pl.pallas_call(
        functools.partial(kernel, dp_count, slab_count, float(voxel_count)),
        out_shape=(
            jax.ShapeDtypeStruct((depth, planes, length), jnp.float32),
            jax.ShapeDtypeStruct((1, channels), jnp.float32),
        ),
        in_specs=[smem, smem, smem, hbm, hbm, hbm, hbm],
        out_specs=(hbm, vmem),
        scratch_shapes=[
            pltpu.VMEM((channels, depth, planes, length), jnp.bfloat16),
            pltpu.VMEM((depth, planes, length), jnp.bfloat16),
            pltpu.VMEM((length, length), jnp.int32),
            pltpu.VMEM((8, length, length), jnp.bfloat16),
            pltpu.VMEM((depth, planes, length), jnp.float32),
            pltpu.VMEM((planes, depth, length), jnp.float32),
            pltpu.VMEM((length, length), jnp.float32),
            pltpu.VMEM((length, length), jnp.float32),
            pltpu.VMEM((length, length), jnp.float32),
            pltpu.VMEM((planes, depth, length), jnp.float32),
            pltpu.VMEM((channels, 8, 128), jnp.float32),
            pltpu.VMEM((2, 1, channels), jnp.float32),
            pltpu.VMEM((slab_count, 1, channels), jnp.float32),
            pltpu.VMEM((dp_count, 1, channels), jnp.float32),
            dma((pieces,)),
            dma((4,)),
            dma((slab_count - 1, pieces)),
            dma((slab_count - 1, pieces)),
            dma((slab_count - 1, pieces)),
            dma((slab_count - 1, pieces)),
            dma((slab_count - 1,)),
            dma((slab_count - 1,)),
            dma((max(dp_count - 1, 1),)),
            dma((max(dp_count - 1, 1),)),
        ],
        compiler_params=pltpu.CompilerParams(
            collective_id=0, has_side_effects=True, vmem_limit_bytes=56 * 1024 * 1024
        ),
    )(
        out_weight, rotation, blocks.T, features[0], target[0], wedge, jnp.asarray(hartley_tables(length)),
    )
    vol_grad, w_grad = pl.pallas_call(
        hand_over,
        out_shape=(
            jax.ShapeDtypeStruct(vol_grad.shape, jnp.float32),
            jax.ShapeDtypeStruct(w_grad.shape, jnp.float32),
        ),
        in_specs=[vmem, vmem],
        out_specs=(vmem, vmem),
    )(vol_grad, w_grad)
    return vol_grad[None], w_grad[0]


def solution(mesh):
    def on_device(features, *rest):
        samples, _, depth, planes, length = features.shape
        whole_planes = (
            samples == 1
            and planes == 8
            and planes == mesh.shape["slab"]
            and depth % ROWS == 0
            and length % 128 == 0
        )
        return (split_planes if whole_planes else split_lines)(features, *rest)

    in_specs = (
        P("dp", None, "slab", None, None),
        P("dp", "slab", None, None),
        P(),
        P("dp"),
        P(),
        P(),
    )
    out_specs = (P("dp", "slab", None, None), P())
    return jax.shard_map(
        on_device, mesh=mesh, in_specs=in_specs, out_specs=out_specs, check_vma=False
    )
```

```python
import functools
import math

import numpy as np

import jax
import jax.numpy as jnp
from jax import lax
from jax.experimental import pallas as pl
from jax.experimental.pallas import tpu as pltpu
from jax.sharding import PartitionSpec as P

BLK = 64
ROWS = 8
HELD = 2
MESH = pl.DeviceIdType.MESH


def product(form, left, right):
    return jnp.einsum(form, left, right, precision=lax.Precision.HIGHEST)


def wedge_weights(blocks, wedge, length):
    per_side = length // BLK
    labels = jnp.arange(per_side, dtype=jnp.int32)
    match = (blocks[:, 0][:, None, None] == labels[None, :, None]) & (
        blocks[:, 1][:, None, None] == labels[None, None, :]
    )
    listed = jnp.any(match, axis=0)
    spread = jnp.repeat(jnp.repeat(listed, BLK, axis=0), BLK, axis=1)
    return jnp.where(spread, wedge, 0).astype(jnp.float32)


def phase_tables(turns, length):
    positions = jnp.arange(length, dtype=jnp.int32)
    flip_depth = turns >= 2
    flip_width = (turns == 1) | (turns == 2)
    depth_index = jnp.where(
        flip_depth[:, None], length - 1 - positions[None, :], positions[None, :]
    )
    width_index = jnp.where(
        flip_width[:, None], length - 1 - positions[None, :], positions[None, :]
    )
    depth_phase = positions[None, :, None] * depth_index[:, None, :] % length
    width_phase = width_index[:, :, None] * positions[None, None, :] % length
    depth_angle = depth_phase.astype(jnp.float32) * (2.0 * math.pi / length)
    width_angle = width_phase.astype(jnp.float32) * (2.0 * math.pi / length)
    return (jnp.cos(depth_angle), jnp.sin(depth_angle), jnp.cos(width_angle), jnp.sin(width_angle))


def split_lines(features, target, out_weight, rotation, blocks, wedge):
    length = features.shape[-1]
    plane_count = features.shape[3]
    slab_count = lax.axis_size("slab")
    columns = length // slab_count
    col_start = lax.axis_index("slab") * columns
    features_wide = features.astype(jnp.float32)
    volume = product("c,sczyx->szyx", out_weight, features_wide)
    difference = volume - target.astype(jnp.float32)
    depth_cos, depth_sin, width_cos, width_sin = phase_tables(rotation, length)
    line_real = product("szyb,sbp->szyp", difference, width_cos)
    line_imag = -product("szyb,sbp->szyp", difference, width_sin)
    line_real, line_imag = (
        lax.all_to_all(line_real, "slab", split_axis=3, concat_axis=1, tiled=True),
        lax.all_to_all(line_imag, "slab", split_axis=3, concat_axis=1, tiled=True),
    )
    spec_real = (
        product("spa,sayq->spyq", depth_cos, line_real)
        + product("spa,sayq->spyq", depth_sin, line_imag)
    ) / length
    spec_imag = (
        product("spa,sayq->spyq", depth_cos, line_imag)
        - product("spa,sayq->spyq", depth_sin, line_real)
    ) / length
    mask = wedge_weights(blocks, wedge, length)
    odd_turn = rotation % 2 == 1
    mask_turned = jnp.where(odd_turn[:, None, None], mask.T[None], mask[None])
    mask_columns = lax.dynamic_slice_in_dim(mask_turned, col_start, columns, 2)
    grad_real = 2.0 * mask_columns[:, :, None, :] * spec_real
    grad_imag = 2.0 * mask_columns[:, :, None, :] * spec_imag
    back_real = product("spa,spyq->sayq", depth_cos, grad_real) - product(
        "spa,spyq->sayq", depth_sin, grad_imag
    )
    back_imag = product("spa,spyq->sayq", depth_cos, grad_imag) + product(
        "spa,spyq->sayq", depth_sin, grad_real
    )
    back_real, back_imag = (
        lax.all_to_all(back_real, "slab", split_axis=1, concat_axis=3, tiled=True),
        lax.all_to_all(back_imag, "slab", split_axis=1, concat_axis=3, tiled=True),
    )
    vol_grad = (
        product("sayp,sbp->sayb", back_real, width_cos)
        - product("sayp,sbp->sayb", back_imag, width_sin)
    ) / length
    voxel_count = lax.axis_size("dp") * features.shape[0] * length * plane_count * length
    local_sum = product("sczyx,szyx->c", features_wide, vol_grad) / voxel_count
    w_grad = lax.psum(local_sum, ("dp", "slab"))
    return (vol_grad, w_grad)


def hartley_tables(length):
    index = np.arange(length)
    angle = (index[:, None] * index[None, :] % length) * (2.0 * np.pi / length)
    cos, sin = np.cos(angle), np.sin(angle)
    parts = []
    for table in (cos, sin, cos + sin, cos - sin):
        high = table.astype(jnp.bfloat16)
        parts += [high, (table - high.astype(np.float64)).astype(jnp.bfloat16)]
    return np.stack(parts)


def halves(value):
    high = value.astype(jnp.bfloat16)
    return high, (value - high.astype(jnp.float32)).astype(jnp.bfloat16)


def dot(left, right):
    return jnp.dot(left, right, preferred_element_type=jnp.float32)


def dot3(left, right):
    return dot(left[0], right[0]) + (dot(left[0], right[1]) + dot(left[1], right[0]))


def kernel(
    dp_count, slab_count, voxel_count,
    weight, rotation, blocks, features_hbm, target_hbm, wedge_hbm, tables_hbm,
    out_hbm, out_sums,
    features, target, wedge, tables, out, outgoing, plane, filt, back, returned, sums, own_sum, all_sums,
    load_sem, side_sem, send_sem, recv_sem, send2_sem, recv2_sem, sum_send_sem, sum_recv_sem,
):
    channels, depth, planes, length = features.shape
    pieces = depth // ROWS
    my_dp, me = lax.axis_index("dp"), lax.axis_index("slab")
    slab_steps = range(slab_count - 1, 0, -1)

    def slab_peer(step):
        return lax.bitwise_xor(me, jnp.int32(step))

    def dp_peer(step):
        return lax.rem(my_dp + step, dp_count)

    loads = []
    for j in range(pieces):
        rows = pl.ds(j * ROWS, ROWS)
        loads.append(pltpu.make_async_copy(features_hbm.at[:, rows], features.at[:, rows], load_sem.at[j]))
    sides = [
        pltpu.make_async_copy(target_hbm, target, side_sem.at[0]),
        pltpu.make_async_copy(wedge_hbm, wedge, side_sem.at[1]),
        pltpu.make_async_copy(tables_hbm, tables, side_sem.at[2]),
    ]
    sides[0].start()
    for copy in loads:
        copy.start()
    for copy in sides[1:]:
        copy.start()

    barrier = pltpu.get_barrier_semaphore()
    for r in slab_steps:
        pl.semaphore_signal(barrier, inc=1, device_id=(my_dp, slab_peer(r)), device_id_type=MESH)
    for r in range(1, dp_count):
        pl.semaphore_signal(barrier, inc=1, device_id=(dp_peer(r), me), device_id_type=MESH)

    sends = []
    for j in range(pieces):
        loads[j].wait()
        if j == 0:
            sides[0].wait()
        base = j * ROWS

        def add_channel(c, accs):
            scale = weight[c]
            return tuple(
                accs[z] + scale * features[c, base + z].astype(jnp.float32) for z in range(ROWS)
            )

        start = tuple(-target[base + z].astype(jnp.float32) for z in range(ROWS))
        accs = lax.fori_loop(0, channels, add_channel, start, unroll=4)
        piece = jnp.swapaxes(jnp.stack(accs, axis=0), 0, 1)
        outgoing[:, pl.ds(base, ROWS), :] = piece
        plane[pl.ds(pl.multiple_of(me * depth + base, ROWS), ROWS), :] = outgoing[me, pl.ds(base, ROWS), :]
        if j < min(HELD, pieces) - 1:
            continue
        first = j
        if j == min(HELD, pieces) - 1:
            pl.semaphore_wait(barrier, slab_count + dp_count - 2)
            first = 0
        rows = pl.ds(first * ROWS, (j + 1 - first) * ROWS)
        for r in slab_steps:
            peer = slab_peer(r)
            copy = pltpu.make_async_remote_copy(
                src_ref=outgoing.at[peer, rows],
                dst_ref=plane.at[pl.ds(pl.multiple_of(me * depth + first * ROWS, ROWS), (j + 1 - first) * ROWS)],
                send_sem=send_sem.at[r - 1, j],
                recv_sem=recv_sem.at[r - 1, j],
                device_id=(my_dp, peer),
                device_id_type=MESH,
            )
            copy.start()
            sends.append(copy)

    sides[1].wait()
    row = lax.broadcasted_iota(jnp.int32, (length, length), 0)
    column = lax.broadcasted_iota(jnp.int32, (length, length), 1)
    row_block, column_block = row // BLK, column // BLK
    listed = jnp.zeros((length, length), jnp.bool_)
    for n in range(blocks.shape[1]):
        listed = listed | ((row_block == blocks[0, n]) & (column_block == blocks[1, n]))
    mask = jnp.where(listed, wedge[...], 0).astype(jnp.float32)
    mirror = jnp.where(lax.rem(row + column, length) == 0, 1.0, 0.0).astype(jnp.bfloat16)
    flipped = dot(dot(mirror, mask.astype(jnp.bfloat16)).astype(jnp.bfloat16), mirror)
    even = mask + flipped
    odd = lax.dot_general(
        even.astype(jnp.bfloat16), mirror, (((0,), (0,)), ((), ())), preferred_element_type=jnp.float32
    )
    is_odd = lax.rem(rotation[0], 2) == 1
    filt[...] = jnp.where(is_odd, odd, even) * (1.0 / (length * length))
    sides[2].wait()

    for copy in sends:
        copy.wait()

    def table(k):
        return tables[2 * k], tables[2 * k + 1]

    values = halves(plane[...])
    first, second = halves(dot3(values, table(2))), halves(dot3(values, table(3)))
    spectrum = dot3(table(0), first) + dot3(table(1), second)
    kept = halves(spectrum * filt[...])
    first, second = halves(dot3(table(0), kept)), halves(dot3(table(1), kept))
    back[...] = dot3(first, table(2)) + dot3(second, table(3))

    sends = []
    for j in range(pieces):
        sends.append([])
        for r in slab_steps:
            peer = slab_peer(r)
            copy = pltpu.make_async_remote_copy(
                src_ref=back.at[pl.ds(pl.multiple_of(peer * depth + j * ROWS, ROWS), ROWS)],
                dst_ref=returned.at[me, pl.ds(j * ROWS, ROWS)],
                send_sem=send2_sem.at[r - 1, j],
                recv_sem=recv2_sem.at[r - 1, j],
                device_id=(my_dp, peer),
                device_id_type=MESH,
            )
            copy.start()
            sends[j].append(copy)
    returned[me] = back[pl.ds(pl.multiple_of(me * depth, ROWS), depth), :]

    for j in range(pieces):
        base = j * ROWS
        for copy in sends[j]:
            copy.wait()
        piece = jnp.swapaxes(returned[:, pl.ds(base, ROWS), :], 0, 1)
        out[pl.ds(base, ROWS)] = piece
        grads = [piece[z] for z in range(ROWS)]

        def channel_sum(c, carry):
            acc = grads[0] * features[c, base].astype(jnp.float32)
            for z in range(1, ROWS):
                acc = acc + grads[z] * features[c, base + z].astype(jnp.float32)
            folded = acc[:, :128]
            for lane in range(128, length, 128):
                folded = folded + acc[:, lane:lane + 128]
            sums[c] = folded if j == 0 else sums[c] + folded
            return carry

        lax.fori_loop(0, channels, channel_sum, 0, unroll=4)
    stored = pltpu.make_async_copy(out, out_hbm, side_sem.at[3])
    stored.start()

    rest = jnp.sum(sums[...], axis=1)
    ones = jnp.ones((8, 128), jnp.bfloat16)
    row_sum = jnp.zeros((8, channels), jnp.float32)
    for _ in range(3):
        part = rest.astype(jnp.bfloat16)
        rest = rest - part.astype(jnp.float32)
        row_sum = row_sum + lax.dot_general(
            ones, part, (((1,), (1,)), ((), ())), preferred_element_type=jnp.float32
        )
    row_sum = row_sum[0:1]
    own_sum[0] = row_sum
    place = my_dp * slab_count + me
    sends = []
    for k in range(dp_count - 1, -1, -1):
        for r in range(slab_count - 1, -1, -1):
            if k == 0 and r == 0:
                continue
            copy = pltpu.make_async_remote_copy(
                src_ref=own_sum.at[0],
                dst_ref=all_sums.at[place],
                send_sem=sum_send_sem.at[k, r],
                recv_sem=sum_recv_sem.at[k, r],
                device_id=(dp_peer(k), slab_peer(r)),
                device_id_type=MESH,
            )
            copy.start()
            sends.append(copy)
    all_sums[place] = row_sum
    for copy in sends:
        copy.wait()
    out_sums[...] = jnp.sum(all_sums[...], axis=0) / voxel_count
    stored.wait()


def hand_over(vol_grad, w_grad, out, out_weight_grad):
    out[...] = vol_grad[...]
    out_weight_grad[...] = w_grad[...]


def split_planes(features, target, out_weight, rotation, blocks, wedge):
    _, channels, depth, planes, length = features.shape
    dp_count, slab_count = lax.axis_size("dp"), lax.axis_size("slab")
    pieces = depth // ROWS
    voxel_count = dp_count * length * planes * length
    smem = pl.BlockSpec(memory_space=pltpu.SMEM)
    hbm = pl.BlockSpec(memory_space=pltpu.HBM)
    vmem = pl.BlockSpec(memory_space=pltpu.VMEM)
    dma = pltpu.SemaphoreType.DMA
    vol_grad, w_grad = pl.pallas_call(
        functools.partial(kernel, dp_count, slab_count, float(voxel_count)),
        out_shape=(
            jax.ShapeDtypeStruct((depth, planes, length), jnp.float32),
            jax.ShapeDtypeStruct((1, channels), jnp.float32),
        ),
        in_specs=[smem, smem, smem, hbm, hbm, hbm, hbm],
        out_specs=(hbm, vmem),
        scratch_shapes=[
            pltpu.VMEM((channels, depth, planes, length), jnp.bfloat16),
            pltpu.VMEM((depth, planes, length), jnp.bfloat16),
            pltpu.VMEM((length, length), jnp.int32),
            pltpu.VMEM((8, length, length), jnp.bfloat16),
            pltpu.VMEM((depth, planes, length), jnp.float32),
            pltpu.VMEM((planes, depth, length), jnp.float32),
            pltpu.VMEM((length, length), jnp.float32),
            pltpu.VMEM((length, length), jnp.float32),
            pltpu.VMEM((length, length), jnp.float32),
            pltpu.VMEM((planes, depth, length), jnp.float32),
            pltpu.VMEM((channels, 8, 128), jnp.float32),
            pltpu.VMEM((1, 1, channels), jnp.float32),
            pltpu.VMEM((dp_count * slab_count, 1, channels), jnp.float32),
            dma((pieces,)),
            dma((4,)),
            dma((slab_count - 1, pieces)),
            dma((slab_count - 1, pieces)),
            dma((slab_count - 1, pieces)),
            dma((slab_count - 1, pieces)),
            dma((dp_count, slab_count)),
            dma((dp_count, slab_count)),
        ],
        compiler_params=pltpu.CompilerParams(
            collective_id=0, has_side_effects=True, vmem_limit_bytes=56 * 1024 * 1024
        ),
    )(
        out_weight, rotation, blocks.T, features[0], target[0], wedge, jnp.asarray(hartley_tables(length)),
    )
    vol_grad, w_grad = pl.pallas_call(
        hand_over,
        out_shape=(
            jax.ShapeDtypeStruct(vol_grad.shape, jnp.float32),
            jax.ShapeDtypeStruct(w_grad.shape, jnp.float32),
        ),
        in_specs=[vmem, vmem],
        out_specs=(vmem, vmem),
    )(vol_grad, w_grad)
    return vol_grad[None], w_grad[0]


def solution(mesh):
    def on_device(features, *rest):
        samples, _, depth, planes, length = features.shape
        whole_planes = (
            samples == 1
            and planes == 8
            and planes == mesh.shape["slab"]
            and depth % ROWS == 0
            and length % 128 == 0
        )
        return (split_planes if whole_planes else split_lines)(features, *rest)

    in_specs = (
        P("dp", None, "slab", None, None),
        P("dp", "slab", None, None),
        P(),
        P("dp"),
        P(),
        P(),
    )
    out_specs = (P("dp", "slab", None, None), P())
    return jax.shard_map(
        on_device, mesh=mesh, in_specs=in_specs, out_specs=out_specs, check_vma=False
    )
```

```python
import functools
import math

import numpy as np

import jax
import jax.numpy as jnp
from jax import lax
from jax.experimental import pallas as pl
from jax.experimental.pallas import tpu as pltpu
from jax.sharding import PartitionSpec as P

BLK = 64
ROWS = 8
HELD = 2
MESH = pl.DeviceIdType.MESH


def product(form, left, right):
    return jnp.einsum(form, left, right, precision=lax.Precision.HIGHEST)


def wedge_weights(blocks, wedge, length):
    per_side = length // BLK
    labels = jnp.arange(per_side, dtype=jnp.int32)
    match = (blocks[:, 0][:, None, None] == labels[None, :, None]) & (
        blocks[:, 1][:, None, None] == labels[None, None, :]
    )
    listed = jnp.any(match, axis=0)
    spread = jnp.repeat(jnp.repeat(listed, BLK, axis=0), BLK, axis=1)
    return jnp.where(spread, wedge, 0).astype(jnp.float32)


def phase_tables(turns, length):
    positions = jnp.arange(length, dtype=jnp.int32)
    flip_depth = turns >= 2
    flip_width = (turns == 1) | (turns == 2)
    depth_index = jnp.where(
        flip_depth[:, None], length - 1 - positions[None, :], positions[None, :]
    )
    width_index = jnp.where(
        flip_width[:, None], length - 1 - positions[None, :], positions[None, :]
    )
    depth_phase = positions[None, :, None] * depth_index[:, None, :] % length
    width_phase = width_index[:, :, None] * positions[None, None, :] % length
    depth_angle = depth_phase.astype(jnp.float32) * (2.0 * math.pi / length)
    width_angle = width_phase.astype(jnp.float32) * (2.0 * math.pi / length)
    return (jnp.cos(depth_angle), jnp.sin(depth_angle), jnp.cos(width_angle), jnp.sin(width_angle))


def split_lines(features, target, out_weight, rotation, blocks, wedge):
    length = features.shape[-1]
    plane_count = features.shape[3]
    slab_count = lax.axis_size("slab")
    columns = length // slab_count
    col_start = lax.axis_index("slab") * columns
    features_wide = features.astype(jnp.float32)
    volume = product("c,sczyx->szyx", out_weight, features_wide)
    difference = volume - target.astype(jnp.float32)
    depth_cos, depth_sin, width_cos, width_sin = phase_tables(rotation, length)
    line_real = product("szyb,sbp->szyp", difference, width_cos)
    line_imag = -product("szyb,sbp->szyp", difference, width_sin)
    line_real, line_imag = (
        lax.all_to_all(line_real, "slab", split_axis=3, concat_axis=1, tiled=True),
        lax.all_to_all(line_imag, "slab", split_axis=3, concat_axis=1, tiled=True),
    )
    spec_real = (
        product("spa,sayq->spyq", depth_cos, line_real)
        + product("spa,sayq->spyq", depth_sin, line_imag)
    ) / length
    spec_imag = (
        product("spa,sayq->spyq", depth_cos, line_imag)
        - product("spa,sayq->spyq", depth_sin, line_real)
    ) / length
    mask = wedge_weights(blocks, wedge, length)
    odd_turn = rotation % 2 == 1
    mask_turned = jnp.where(odd_turn[:, None, None], mask.T[None], mask[None])
    mask_columns = lax.dynamic_slice_in_dim(mask_turned, col_start, columns, 2)
    grad_real = 2.0 * mask_columns[:, :, None, :] * spec_real
    grad_imag = 2.0 * mask_columns[:, :, None, :] * spec_imag
    back_real = product("spa,spyq->sayq", depth_cos, grad_real) - product(
        "spa,spyq->sayq", depth_sin, grad_imag
    )
    back_imag = product("spa,spyq->sayq", depth_cos, grad_imag) + product(
        "spa,spyq->sayq", depth_sin, grad_real
    )
    back_real, back_imag = (
        lax.all_to_all(back_real, "slab", split_axis=1, concat_axis=3, tiled=True),
        lax.all_to_all(back_imag, "slab", split_axis=1, concat_axis=3, tiled=True),
    )
    vol_grad = (
        product("sayp,sbp->sayb", back_real, width_cos)
        - product("sayp,sbp->sayb", back_imag, width_sin)
    ) / length
    voxel_count = lax.axis_size("dp") * features.shape[0] * length * plane_count * length
    local_sum = product("sczyx,szyx->c", features_wide, vol_grad) / voxel_count
    w_grad = lax.psum(local_sum, ("dp", "slab"))
    return (vol_grad, w_grad)


def hartley_tables(length):
    index = np.arange(length)
    angle = (index[:, None] * index[None, :] % length) * (2.0 * np.pi / length)
    cos, sin = np.cos(angle), np.sin(angle)
    parts = []
    for table in (cos, sin, cos + sin, cos - sin):
        high = table.astype(jnp.bfloat16)
        parts += [high, (table - high.astype(np.float64)).astype(jnp.bfloat16)]
    return np.stack(parts)


def halves(value):
    high = value.astype(jnp.bfloat16)
    return high, (value - high.astype(jnp.float32)).astype(jnp.bfloat16)


def dot(left, right):
    return jnp.dot(left, right, preferred_element_type=jnp.float32)


def dot3(left, right):
    return dot(left[0], right[0]) + (dot(left[0], right[1]) + dot(left[1], right[0]))


def kernel(
    dp_count, slab_count, voxel_count,
    weight, rotation, blocks, features_hbm, target_hbm, wedge_hbm, tables_hbm,
    out_hbm, out_sums,
    features, target, wedge, tables, out, outgoing, plane, filt, back, returned, sums, own_sum, all_sums,
    load_sem, side_sem, send_sem, recv_sem, send2_sem, recv2_sem, sum_send_sem, sum_recv_sem,
):
    channels, depth, planes, length = features.shape
    pieces = depth // ROWS
    my_dp, me = lax.axis_index("dp"), lax.axis_index("slab")
    slab_steps = range(slab_count - 1, 0, -1)

    def slab_peer(step):
        return lax.bitwise_xor(me, jnp.int32(step))

    def dp_peer(step):
        return lax.rem(my_dp + step, dp_count)

    loads = []
    for j in range(pieces):
        rows = pl.ds(j * ROWS, ROWS)
        loads.append(pltpu.make_async_copy(features_hbm.at[:, rows], features.at[:, rows], load_sem.at[j]))
    sides = [
        pltpu.make_async_copy(target_hbm, target, side_sem.at[0]),
        pltpu.make_async_copy(wedge_hbm, wedge, side_sem.at[1]),
        pltpu.make_async_copy(tables_hbm, tables, side_sem.at[2]),
    ]
    sides[0].start()
    for copy in loads:
        copy.start()
    for copy in sides[1:]:
        copy.start()

    barrier = pltpu.get_barrier_semaphore()
    for r in slab_steps:
        pl.semaphore_signal(barrier, inc=1, device_id=(my_dp, slab_peer(r)), device_id_type=MESH)
    for r in range(1, dp_count):
        pl.semaphore_signal(barrier, inc=1, device_id=(dp_peer(r), me), device_id_type=MESH)

    sends = []
    for j in range(pieces):
        loads[j].wait()
        if j == 0:
            sides[0].wait()
        base = j * ROWS

        def add_channel(c, accs):
            scale = weight[c]
            return tuple(
                accs[z] + scale * features[c, base + z].astype(jnp.float32) for z in range(ROWS)
            )

        start = tuple(-target[base + z].astype(jnp.float32) for z in range(ROWS))
        accs = lax.fori_loop(0, channels, add_channel, start, unroll=4)
        piece = jnp.swapaxes(jnp.stack(accs, axis=0), 0, 1)
        outgoing[:, pl.ds(base, ROWS), :] = piece
        plane[pl.ds(pl.multiple_of(me * depth + base, ROWS), ROWS), :] = outgoing[me, pl.ds(base, ROWS), :]
        if j < min(HELD, pieces) - 1:
            continue
        first = j
        if j == min(HELD, pieces) - 1:
            pl.semaphore_wait(barrier, slab_count + dp_count - 2)
            first = 0
        rows = pl.ds(first * ROWS, (j + 1 - first) * ROWS)
        for r in slab_steps:
            peer = slab_peer(r)
            copy = pltpu.make_async_remote_copy(
                src_ref=outgoing.at[peer, rows],
                dst_ref=plane.at[pl.ds(pl.multiple_of(me * depth + first * ROWS, ROWS), (j + 1 - first) * ROWS)],
                send_sem=send_sem.at[r - 1, j],
                recv_sem=recv_sem.at[r - 1, j],
                device_id=(my_dp, peer),
                device_id_type=MESH,
            )
            copy.start()
            sends.append(copy)

    sides[1].wait()
    row = lax.broadcasted_iota(jnp.int32, (length, length), 0)
    column = lax.broadcasted_iota(jnp.int32, (length, length), 1)
    row_block, column_block = row // BLK, column // BLK
    listed = jnp.zeros((length, length), jnp.bool_)
    for n in range(blocks.shape[1]):
        listed = listed | ((row_block == blocks[0, n]) & (column_block == blocks[1, n]))
    mask = jnp.where(listed, wedge[...], 0).astype(jnp.float32)
    mirror = jnp.where(lax.rem(row + column, length) == 0, 1.0, 0.0).astype(jnp.bfloat16)
    flipped = dot(dot(mirror, mask.astype(jnp.bfloat16)).astype(jnp.bfloat16), mirror)
    even = mask + flipped
    odd = lax.dot_general(
        even.astype(jnp.bfloat16), mirror, (((0,), (0,)), ((), ())), preferred_element_type=jnp.float32
    )
    is_odd = lax.rem(rotation[0], 2) == 1
    filt[...] = jnp.where(is_odd, odd, even) * (1.0 / (length * length))
    sides[2].wait()

    for copy in sends:
        copy.wait()

    def table(k):
        return tables[2 * k], tables[2 * k + 1]

    values = halves(plane[...])
    first, second = halves(dot3(values, table(2))), halves(dot3(values, table(3)))
    spectrum = dot3(table(0), first) + dot3(table(1), second)
    kept = halves(spectrum * filt[...])

    half = depth // 2

    def table_rows(k, h):
        return tuple(
            part.reshape(slab_count, 2, half, length)[:, h].reshape(slab_count * half, length) for part in table(k)
        )

    sends = []
    for h in range(2):
        first = halves(dot3(table_rows(0, h), kept))
        second = halves(dot3(table_rows(1, h), kept))
        rows = dot3(first, table(2)) + dot3(second, table(3))
        back[:, pl.ds(h * half, half), :] = rows.reshape(slab_count, half, length)
        for j in range(h * pieces // 2, (h + 1) * pieces // 2):
            sends.append([])
            for r in slab_steps:
                peer = slab_peer(r)
                copy = pltpu.make_async_remote_copy(
                    src_ref=back.at[peer, pl.ds(j * ROWS, ROWS)],
                    dst_ref=returned.at[me, pl.ds(j * ROWS, ROWS)],
                    send_sem=send2_sem.at[r - 1, j],
                    recv_sem=recv2_sem.at[r - 1, j],
                    device_id=(my_dp, peer),
                    device_id_type=MESH,
                )
                copy.start()
                sends[j].append(copy)
    returned[me] = back[me]

    for j in range(pieces):
        base = j * ROWS
        for copy in sends[j]:
            copy.wait()
        piece = jnp.swapaxes(returned[:, pl.ds(base, ROWS), :], 0, 1)
        out[pl.ds(base, ROWS)] = piece
        grads = [piece[z] for z in range(ROWS)]

        def channel_sum(c, carry):
            acc = grads[0] * features[c, base].astype(jnp.float32)
            for z in range(1, ROWS):
                acc = acc + grads[z] * features[c, base + z].astype(jnp.float32)
            folded = acc[:, :128]
            for lane in range(128, length, 128):
                folded = folded + acc[:, lane:lane + 128]
            sums[c] = folded if j == 0 else sums[c] + folded
            return carry

        lax.fori_loop(0, channels, channel_sum, 0, unroll=4)
    stored = pltpu.make_async_copy(out, out_hbm, side_sem.at[3])
    stored.start()

    rest = jnp.sum(sums[...], axis=1)
    ones = jnp.ones((8, 128), jnp.bfloat16)
    row_sum = jnp.zeros((8, channels), jnp.float32)
    for _ in range(3):
        part = rest.astype(jnp.bfloat16)
        rest = rest - part.astype(jnp.float32)
        row_sum = row_sum + lax.dot_general(
            ones, part, (((1,), (1,)), ((), ())), preferred_element_type=jnp.float32
        )
    row_sum = row_sum[0:1]
    own_sum[0] = row_sum
    place = my_dp * slab_count + me
    sends = []
    for k in range(dp_count - 1, -1, -1):
        for r in range(slab_count - 1, -1, -1):
            if k == 0 and r == 0:
                continue
            copy = pltpu.make_async_remote_copy(
                src_ref=own_sum.at[0],
                dst_ref=all_sums.at[place],
                send_sem=sum_send_sem.at[k, r],
                recv_sem=sum_recv_sem.at[k, r],
                device_id=(dp_peer(k), slab_peer(r)),
                device_id_type=MESH,
            )
            copy.start()
            sends.append(copy)
    all_sums[place] = row_sum
    for copy in sends:
        copy.wait()
    out_sums[...] = jnp.sum(all_sums[...], axis=0) / voxel_count
    stored.wait()


def hand_over(vol_grad, w_grad, out, out_weight_grad):
    out[...] = vol_grad[...]
    out_weight_grad[...] = w_grad[...]


def split_planes(features, target, out_weight, rotation, blocks, wedge):
    _, channels, depth, planes, length = features.shape
    dp_count, slab_count = lax.axis_size("dp"), lax.axis_size("slab")
    pieces = depth // ROWS
    voxel_count = dp_count * length * planes * length
    smem = pl.BlockSpec(memory_space=pltpu.SMEM)
    hbm = pl.BlockSpec(memory_space=pltpu.HBM)
    vmem = pl.BlockSpec(memory_space=pltpu.VMEM)
    dma = pltpu.SemaphoreType.DMA
    vol_grad, w_grad = pl.pallas_call(
        functools.partial(kernel, dp_count, slab_count, float(voxel_count)),
        out_shape=(
            jax.ShapeDtypeStruct((depth, planes, length), jnp.float32),
            jax.ShapeDtypeStruct((1, channels), jnp.float32),
        ),
        in_specs=[smem, smem, smem, hbm, hbm, hbm, hbm],
        out_specs=(hbm, vmem),
        scratch_shapes=[
            pltpu.VMEM((channels, depth, planes, length), jnp.bfloat16),
            pltpu.VMEM((depth, planes, length), jnp.bfloat16),
            pltpu.VMEM((length, length), jnp.int32),
            pltpu.VMEM((8, length, length), jnp.bfloat16),
            pltpu.VMEM((depth, planes, length), jnp.float32),
            pltpu.VMEM((planes, depth, length), jnp.float32),
            pltpu.VMEM((length, length), jnp.float32),
            pltpu.VMEM((length, length), jnp.float32),
            pltpu.VMEM((slab_count, depth, length), jnp.float32),
            pltpu.VMEM((planes, depth, length), jnp.float32),
            pltpu.VMEM((channels, 8, 128), jnp.float32),
            pltpu.VMEM((1, 1, channels), jnp.float32),
            pltpu.VMEM((dp_count * slab_count, 1, channels), jnp.float32),
            dma((pieces,)),
            dma((4,)),
            dma((slab_count - 1, pieces)),
            dma((slab_count - 1, pieces)),
            dma((slab_count - 1, pieces)),
            dma((slab_count - 1, pieces)),
            dma((dp_count, slab_count)),
            dma((dp_count, slab_count)),
        ],
        compiler_params=pltpu.CompilerParams(
            collective_id=0, has_side_effects=True, vmem_limit_bytes=56 * 1024 * 1024
        ),
    )(
        out_weight, rotation, blocks.T, features[0], target[0], wedge, jnp.asarray(hartley_tables(length)),
    )
    vol_grad, w_grad = pl.pallas_call(
        hand_over,
        out_shape=(
            jax.ShapeDtypeStruct(vol_grad.shape, jnp.float32),
            jax.ShapeDtypeStruct(w_grad.shape, jnp.float32),
        ),
        in_specs=[vmem, vmem],
        out_specs=(vmem, vmem),
    )(vol_grad, w_grad)
    return vol_grad[None], w_grad[0]


def solution(mesh):
    def on_device(features, *rest):
        samples, _, depth, planes, length = features.shape
        whole_planes = (
            samples == 1
            and planes == 8
            and planes == mesh.shape["slab"]
            and depth % (4 * ROWS) == 0
            and length % 128 == 0
        )
        return (split_planes if whole_planes else split_lines)(features, *rest)

    in_specs = (
        P("dp", None, "slab", None, None),
        P("dp", "slab", None, None),
        P(),
        P("dp"),
        P(),
        P(),
    )
    out_specs = (P("dp", "slab", None, None), P())
    return jax.shard_map(
        on_device, mesh=mesh, in_specs=in_specs, out_specs=out_specs, check_vma=False
    )
```

```python
import functools
import math

import numpy as np

import jax
import jax.numpy as jnp
from jax import lax
from jax.experimental import pallas as pl
from jax.experimental.pallas import tpu as pltpu
from jax.sharding import PartitionSpec as P

BLK = 64
ROWS = 8
HELD = 2
MESH = pl.DeviceIdType.MESH


def product(form, left, right):
    return jnp.einsum(form, left, right, precision=lax.Precision.HIGHEST)


def wedge_weights(blocks, wedge, length):
    per_side = length // BLK
    labels = jnp.arange(per_side, dtype=jnp.int32)
    match = (blocks[:, 0][:, None, None] == labels[None, :, None]) & (
        blocks[:, 1][:, None, None] == labels[None, None, :]
    )
    listed = jnp.any(match, axis=0)
    spread = jnp.repeat(jnp.repeat(listed, BLK, axis=0), BLK, axis=1)
    return jnp.where(spread, wedge, 0).astype(jnp.float32)


def phase_tables(turns, length):
    positions = jnp.arange(length, dtype=jnp.int32)
    flip_depth = turns >= 2
    flip_width = (turns == 1) | (turns == 2)
    depth_index = jnp.where(
        flip_depth[:, None], length - 1 - positions[None, :], positions[None, :]
    )
    width_index = jnp.where(
        flip_width[:, None], length - 1 - positions[None, :], positions[None, :]
    )
    depth_phase = positions[None, :, None] * depth_index[:, None, :] % length
    width_phase = width_index[:, :, None] * positions[None, None, :] % length
    depth_angle = depth_phase.astype(jnp.float32) * (2.0 * math.pi / length)
    width_angle = width_phase.astype(jnp.float32) * (2.0 * math.pi / length)
    return (jnp.cos(depth_angle), jnp.sin(depth_angle), jnp.cos(width_angle), jnp.sin(width_angle))


def split_lines(features, target, out_weight, rotation, blocks, wedge):
    length = features.shape[-1]
    plane_count = features.shape[3]
    slab_count = lax.axis_size("slab")
    columns = length // slab_count
    col_start = lax.axis_index("slab") * columns
    features_wide = features.astype(jnp.float32)
    volume = product("c,sczyx->szyx", out_weight, features_wide)
    difference = volume - target.astype(jnp.float32)
    depth_cos, depth_sin, width_cos, width_sin = phase_tables(rotation, length)
    line_real = product("szyb,sbp->szyp", difference, width_cos)
    line_imag = -product("szyb,sbp->szyp", difference, width_sin)
    line_real, line_imag = (
        lax.all_to_all(line_real, "slab", split_axis=3, concat_axis=1, tiled=True),
        lax.all_to_all(line_imag, "slab", split_axis=3, concat_axis=1, tiled=True),
    )
    spec_real = (
        product("spa,sayq->spyq", depth_cos, line_real)
        + product("spa,sayq->spyq", depth_sin, line_imag)
    ) / length
    spec_imag = (
        product("spa,sayq->spyq", depth_cos, line_imag)
        - product("spa,sayq->spyq", depth_sin, line_real)
    ) / length
    mask = wedge_weights(blocks, wedge, length)
    odd_turn = rotation % 2 == 1
    mask_turned = jnp.where(odd_turn[:, None, None], mask.T[None], mask[None])
    mask_columns = lax.dynamic_slice_in_dim(mask_turned, col_start, columns, 2)
    grad_real = 2.0 * mask_columns[:, :, None, :] * spec_real
    grad_imag = 2.0 * mask_columns[:, :, None, :] * spec_imag
    back_real = product("spa,spyq->sayq", depth_cos, grad_real) - product(
        "spa,spyq->sayq", depth_sin, grad_imag
    )
    back_imag = product("spa,spyq->sayq", depth_cos, grad_imag) + product(
        "spa,spyq->sayq", depth_sin, grad_real
    )
    back_real, back_imag = (
        lax.all_to_all(back_real, "slab", split_axis=1, concat_axis=3, tiled=True),
        lax.all_to_all(back_imag, "slab", split_axis=1, concat_axis=3, tiled=True),
    )
    vol_grad = (
        product("sayp,sbp->sayb", back_real, width_cos)
        - product("sayp,sbp->sayb", back_imag, width_sin)
    ) / length
    voxel_count = lax.axis_size("dp") * features.shape[0] * length * plane_count * length
    local_sum = product("sczyx,szyx->c", features_wide, vol_grad) / voxel_count
    w_grad = lax.psum(local_sum, ("dp", "slab"))
    return (vol_grad, w_grad)


def hartley_tables(length):
    index = np.arange(length)
    angle = (index[:, None] * index[None, :] % length) * (2.0 * np.pi / length)
    cos, sin = np.cos(angle), np.sin(angle)
    parts = []
    for table in (cos, sin, cos + sin, cos - sin):
        high = table.astype(jnp.bfloat16)
        parts += [high, (table - high.astype(np.float64)).astype(jnp.bfloat16)]
    return np.stack(parts)


def halves(value):
    high = value.astype(jnp.bfloat16)
    return high, (value - high.astype(jnp.float32)).astype(jnp.bfloat16)


def dot(left, right):
    return jnp.dot(left, right, preferred_element_type=jnp.float32)


def dot3(left, right):
    return dot(left[0], right[0]) + (dot(left[0], right[1]) + dot(left[1], right[0]))


def kernel(
    dp_count, slab_count, voxel_count,
    weight, rotation, blocks, features_hbm, target_hbm, wedge_hbm, tables_hbm,
    out_hbm, out_sums,
    features, target, wedge, tables, out, outgoing, plane, filt, back, returned, sums, own_sum, all_sums,
    load_sem, side_sem, send_sem, recv_sem, send2_sem, recv2_sem, sum_send_sem, sum_recv_sem,
):
    channels, depth, planes, length = features.shape
    pieces = depth // ROWS
    my_dp, me = lax.axis_index("dp"), lax.axis_index("slab")
    slab_steps = range(slab_count - 1, 0, -1)

    def slab_peer(step):
        return lax.bitwise_xor(me, jnp.int32(step))

    def dp_peer(step):
        return lax.rem(my_dp + step, dp_count)

    loads = []
    for j in range(pieces):
        rows = pl.ds(j * ROWS, ROWS)
        loads.append(pltpu.make_async_copy(features_hbm.at[:, rows], features.at[:, rows], load_sem.at[j]))
    sides = [
        pltpu.make_async_copy(target_hbm, target, side_sem.at[0]),
        pltpu.make_async_copy(wedge_hbm, wedge, side_sem.at[1]),
        pltpu.make_async_copy(tables_hbm, tables, side_sem.at[2]),
    ]
    sides[0].start()
    for copy in loads:
        copy.start()
    for copy in sides[1:]:
        copy.start()

    barrier = pltpu.get_barrier_semaphore()
    for r in slab_steps:
        pl.semaphore_signal(barrier, inc=1, device_id=(my_dp, slab_peer(r)), device_id_type=MESH)
    for r in range(1, dp_count):
        pl.semaphore_signal(barrier, inc=1, device_id=(dp_peer(r), me), device_id_type=MESH)

    sends = []
    for j in range(pieces):
        loads[j].wait()
        if j == 0:
            sides[0].wait()
        base = j * ROWS

        def add_channel(c, accs):
            scale = weight[c]
            return tuple(
                accs[z] + scale * features[c, base + z].astype(jnp.float32) for z in range(ROWS)
            )

        start = tuple(-target[base + z].astype(jnp.float32) for z in range(ROWS))
        accs = lax.fori_loop(0, channels, add_channel, start, unroll=4)
        piece = jnp.swapaxes(jnp.stack(accs, axis=0), 0, 1)
        outgoing[:, pl.ds(base, ROWS), :] = piece
        plane[pl.ds(pl.multiple_of(me * depth + base, ROWS), ROWS), :] = outgoing[me, pl.ds(base, ROWS), :]
        if j < min(HELD, pieces) - 1:
            continue
        first = j
        if j == min(HELD, pieces) - 1:
            pl.semaphore_wait(barrier, slab_count + dp_count - 2)
            first = 0
        rows = pl.ds(first * ROWS, (j + 1 - first) * ROWS)
        for r in slab_steps:
            peer = slab_peer(r)
            copy = pltpu.make_async_remote_copy(
                src_ref=outgoing.at[peer, rows],
                dst_ref=plane.at[pl.ds(pl.multiple_of(me * depth + first * ROWS, ROWS), (j + 1 - first) * ROWS)],
                send_sem=send_sem.at[r - 1, j],
                recv_sem=recv_sem.at[r - 1, j],
                device_id=(my_dp, peer),
                device_id_type=MESH,
            )
            copy.start()
            sends.append(copy)

    sides[1].wait()
    row = lax.broadcasted_iota(jnp.int32, (length, length), 0)
    column = lax.broadcasted_iota(jnp.int32, (length, length), 1)
    row_block, column_block = row // BLK, column // BLK
    listed = jnp.zeros((length, length), jnp.bool_)
    for n in range(blocks.shape[1]):
        listed = listed | ((row_block == blocks[0, n]) & (column_block == blocks[1, n]))
    mask = jnp.where(listed, wedge[...], 0).astype(jnp.float32)
    mirror = jnp.where(lax.rem(row + column, length) == 0, 1.0, 0.0).astype(jnp.bfloat16)
    flipped = dot(dot(mirror, mask.astype(jnp.bfloat16)).astype(jnp.bfloat16), mirror)
    even = mask + flipped
    odd = lax.dot_general(
        even.astype(jnp.bfloat16), mirror, (((0,), (0,)), ((), ())), preferred_element_type=jnp.float32
    )
    is_odd = lax.rem(rotation[0], 2) == 1
    filt[...] = jnp.where(is_odd, odd, even) * (1.0 / (length * length))
    sides[2].wait()

    def table(k):
        return tables[2 * k], tables[2 * k + 1]

    half = depth // 2
    lines = []
    for h in range(2):
        for copy in sends[:slab_count - 1] if h == 0 else sends[slab_count - 1:]:
            copy.wait()
        values = halves(jnp.concatenate(
            [plane[q * depth + h * half:q * depth + (h + 1) * half, :] for q in range(slab_count)], axis=0
        ))
        lines.append([dot3(values, table(k)).reshape(slab_count, half, length) for k in (2, 3)])
    first, second = (
        halves(jnp.stack([lines[0][k], lines[1][k]], axis=1).reshape(length, length)) for k in range(2)
    )
    spectrum = dot3(table(0), first) + dot3(table(1), second)
    kept = halves(spectrum * filt[...])

    def table_rows(k, h):
        return tuple(
            part.reshape(slab_count, 2, half, length)[:, h].reshape(slab_count * half, length) for part in table(k)
        )

    sends = []
    for h in range(2):
        first = halves(dot3(table_rows(0, h), kept))
        second = halves(dot3(table_rows(1, h), kept))
        rows = dot3(first, table(2)) + dot3(second, table(3))
        back[:, pl.ds(h * half, half), :] = rows.reshape(slab_count, half, length)
        for j in range(h * pieces // 2, (h + 1) * pieces // 2):
            sends.append([])
            for r in slab_steps:
                peer = slab_peer(r)
                copy = pltpu.make_async_remote_copy(
                    src_ref=back.at[peer, pl.ds(j * ROWS, ROWS)],
                    dst_ref=returned.at[me, pl.ds(j * ROWS, ROWS)],
                    send_sem=send2_sem.at[r - 1, j],
                    recv_sem=recv2_sem.at[r - 1, j],
                    device_id=(my_dp, peer),
                    device_id_type=MESH,
                )
                copy.start()
                sends[j].append(copy)
    returned[me] = back[me]

    for j in range(pieces):
        base = j * ROWS
        for copy in sends[j]:
            copy.wait()
        piece = jnp.swapaxes(returned[:, pl.ds(base, ROWS), :], 0, 1)
        out[pl.ds(base, ROWS)] = piece
        grads = [piece[z] for z in range(ROWS)]

        def channel_sum(c, carry):
            acc = grads[0] * features[c, base].astype(jnp.float32)
            for z in range(1, ROWS):
                acc = acc + grads[z] * features[c, base + z].astype(jnp.float32)
            folded = acc[:, :128]
            for lane in range(128, length, 128):
                folded = folded + acc[:, lane:lane + 128]
            sums[c] = folded if j == 0 else sums[c] + folded
            return carry

        lax.fori_loop(0, channels, channel_sum, 0, unroll=4)
    stored = pltpu.make_async_copy(out, out_hbm, side_sem.at[3])
    stored.start()

    rest = jnp.sum(sums[...], axis=1)
    ones = jnp.ones((8, 128), jnp.bfloat16)
    row_sum = jnp.zeros((8, channels), jnp.float32)
    for _ in range(3):
        part = rest.astype(jnp.bfloat16)
        rest = rest - part.astype(jnp.float32)
        row_sum = row_sum + lax.dot_general(
            ones, part, (((1,), (1,)), ((), ())), preferred_element_type=jnp.float32
        )
    row_sum = row_sum[0:1]
    own_sum[0] = row_sum
    place = my_dp * slab_count + me
    sends = []
    for k in range(dp_count - 1, -1, -1):
        for r in range(slab_count - 1, -1, -1):
            if k == 0 and r == 0:
                continue
            copy = pltpu.make_async_remote_copy(
                src_ref=own_sum.at[0],
                dst_ref=all_sums.at[place],
                send_sem=sum_send_sem.at[k, r],
                recv_sem=sum_recv_sem.at[k, r],
                device_id=(dp_peer(k), slab_peer(r)),
                device_id_type=MESH,
            )
            copy.start()
            sends.append(copy)
    all_sums[place] = row_sum
    for copy in sends:
        copy.wait()
    out_sums[...] = jnp.sum(all_sums[...], axis=0) / voxel_count
    stored.wait()


def hand_over(vol_grad, w_grad, out, out_weight_grad):
    out[...] = vol_grad[...]
    out_weight_grad[...] = w_grad[...]


def split_planes(features, target, out_weight, rotation, blocks, wedge):
    _, channels, depth, planes, length = features.shape
    dp_count, slab_count = lax.axis_size("dp"), lax.axis_size("slab")
    pieces = depth // ROWS
    voxel_count = dp_count * length * planes * length
    smem = pl.BlockSpec(memory_space=pltpu.SMEM)
    hbm = pl.BlockSpec(memory_space=pltpu.HBM)
    vmem = pl.BlockSpec(memory_space=pltpu.VMEM)
    dma = pltpu.SemaphoreType.DMA
    vol_grad, w_grad = pl.pallas_call(
        functools.partial(kernel, dp_count, slab_count, float(voxel_count)),
        out_shape=(
            jax.ShapeDtypeStruct((depth, planes, length), jnp.float32),
            jax.ShapeDtypeStruct((1, channels), jnp.float32),
        ),
        in_specs=[smem, smem, smem, hbm, hbm, hbm, hbm],
        out_specs=(hbm, vmem),
        scratch_shapes=[
            pltpu.VMEM((channels, depth, planes, length), jnp.bfloat16),
            pltpu.VMEM((depth, planes, length), jnp.bfloat16),
            pltpu.VMEM((length, length), jnp.int32),
            pltpu.VMEM((8, length, length), jnp.bfloat16),
            pltpu.VMEM((depth, planes, length), jnp.float32),
            pltpu.VMEM((planes, depth, length), jnp.float32),
            pltpu.VMEM((length, length), jnp.float32),
            pltpu.VMEM((length, length), jnp.float32),
            pltpu.VMEM((slab_count, depth, length), jnp.float32),
            pltpu.VMEM((planes, depth, length), jnp.float32),
            pltpu.VMEM((channels, 8, 128), jnp.float32),
            pltpu.VMEM((1, 1, channels), jnp.float32),
            pltpu.VMEM((dp_count * slab_count, 1, channels), jnp.float32),
            dma((pieces,)),
            dma((4,)),
            dma((slab_count - 1, pieces)),
            dma((slab_count - 1, pieces)),
            dma((slab_count - 1, pieces)),
            dma((slab_count - 1, pieces)),
            dma((dp_count, slab_count)),
            dma((dp_count, slab_count)),
        ],
        compiler_params=pltpu.CompilerParams(
            collective_id=0, has_side_effects=True, vmem_limit_bytes=56 * 1024 * 1024
        ),
    )(
        out_weight, rotation, blocks.T, features[0], target[0], wedge, jnp.asarray(hartley_tables(length)),
    )
    vol_grad, w_grad = pl.pallas_call(
        hand_over,
        out_shape=(
            jax.ShapeDtypeStruct(vol_grad.shape, jnp.float32),
            jax.ShapeDtypeStruct(w_grad.shape, jnp.float32),
        ),
        in_specs=[vmem, vmem],
        out_specs=(vmem, vmem),
    )(vol_grad, w_grad)
    return vol_grad[None], w_grad[0]


def solution(mesh):
    def on_device(features, *rest):
        samples, _, depth, planes, length = features.shape
        whole_planes = (
            samples == 1
            and planes == 8
            and planes == mesh.shape["slab"]
            and depth == 2 * HELD * ROWS
            and length % 128 == 0
        )
        return (split_planes if whole_planes else split_lines)(features, *rest)

    in_specs = (
        P("dp", None, "slab", None, None),
        P("dp", "slab", None, None),
        P(),
        P("dp"),
        P(),
        P(),
    )
    out_specs = (P("dp", "slab", None, None), P())
    return jax.shard_map(
        on_device, mesh=mesh, in_specs=in_specs, out_specs=out_specs, check_vma=False
    )
```
